32 devices in a mesh: feed: 8 (over y, x, core), tm: 4 (over z).
Axes of the slice: x: 2, y: 2, z: 4, core: 2. Of those that a mesh axis runs over, the one named last changes fastest.
Arguments:
- voltages: bfloat16 [256, 1048576], P('feed', 'tm'), may hold values from -12 to 12
- filter_taps: float32 [4, 1024], replicated, may hold values from -1 to 1
- delays: float32 [256], P('feed'), may hold values from -64 to 64
- channel_flags: int32 [512], P('feed'), may hold values from 0 to 1, as said below
Outputs:
- visibilities: float32 [512, 256, 256], P(('feed', 'tm'))
The draws below stay inside these ranges and needn't reach their ends.
Inputs may be any that keep to these rules, and one draw needn't show every extreme that they name: `channel_flags`: channel c belongs to owner c // 64; every owner keeps between 16 and 64 of its channels, and in every draw some owner keeps all of them.
All inputs are finite; a program needn't handle non-finite values.
Results may differ from the reference program's by a relative error of at most 0.0011.
Values may be sent and summed in bfloat16 or wider, within the bound.
A program may use at most 192 MiB of HBM per device.

```python
import math
import jax
import jax.numpy as jnp
from jax import lax

NI = 256
NFFT = 1024
TAPS = 4
SOURCES = 4
CHANNEL_COUNT = 512
S_TOT = 1024
CHANNELS_OWNED = 64


def draw_voltages(key, part):
    length = S_TOT * NFFT
    noise_key = jax.random.fold_in(key, 11)
    gain_key = jax.random.fold_in(key, 12)
    signal_key = jax.random.fold_in(key, 13)
    source_gains = jax.random.normal(gain_key, (NI, SOURCES), jnp.float32) * 0.5
    signals = jax.random.normal(signal_key, (SOURCES, length), jnp.float32)
    noise = jax.random.normal(noise_key, (NI, length), jnp.float32)
    result = noise
    for source in range(SOURCES):
        result = result + source_gains[:, source:source + 1] * signals[source][None, :]
    return jnp.clip(result, -12.0, 12.0).astype(jnp.bfloat16)


def draw_channel_flags(key, part):
    owner_total = CHANNEL_COUNT // CHANNELS_OWNED
    clean_channels = jax.random.randint(jax.random.fold_in(key, 21), (owner_total,), CHANNELS_OWNED // 4, CHANNELS_OWNED + 1)
    largest_owner_load = jax.random.randint(jax.random.fold_in(key, 22), (), 0, owner_total)
    clean_channels = jnp.where(jnp.arange(owner_total) == largest_owner_load, CHANNELS_OWNED, clean_channels)
    order_keys = jax.random.split(jax.random.fold_in(key, 23), owner_total)
    channel_orderings = jax.vmap(lambda order_key: jax.random.permutation(order_key, CHANNELS_OWNED))(order_keys)
    return (channel_orderings < clean_channels[:, None]).astype(jnp.int32).reshape(CHANNEL_COUNT)


def block_scale(key, shape, cuts, smallest, largest):
    def one(axis_at, blocks):
        steps = jax.random.uniform(jax.random.fold_in(jax.random.fold_in(key, 6), axis_at), (blocks,), jnp.float32, smallest / len(cuts), largest / len(cuts))
        return jnp.repeat(jnp.exp(steps), shape[axis_at] // blocks).reshape((-1,) + (1,) * (len(shape) - axis_at - 1))

    factor_of = one(*cuts[0])
    for cut in cuts[1:]:
        factor_of = factor_of * one(*cut)
    return factor_of


def setup_inputs(seed: int = 0) -> dict:
    key_of = jax.random.split(jax.random.key(seed), 5)
    voltages = draw_voltages(jax.random.fold_in(key_of[4], 71), 0)
    filter_taps = jnp.clip(jax.random.uniform(key_of[1], (TAPS, NFFT), jnp.float32, -1.0, 1.0), -1.0, 1.0)
    delays = jnp.clip(jax.random.uniform(key_of[2], (NI,), jnp.float32, -64.0, 64.0) * block_scale(key_of[2], (NI,), ((0, 8),), -0.4, 0.0), -64.0, 64.0)
    channel_flags = draw_channel_flags(jax.random.fold_in(key_of[4], 71), 0)
    return {"voltages": voltages, "filter_taps": filter_taps, "delays": delays, "channel_flags": channel_flags}


def build_table(fft_length):
    channels = jnp.arange(fft_length // 2, dtype=jnp.int32)
    samples = jnp.arange(fft_length, dtype=jnp.int32)
    product = channels[:, None] * samples[None, :] % fft_length
    angles = product.astype(jnp.float32) * (2.0 * math.pi / fft_length)
    return jnp.stack([jnp.cos(angles), -jnp.sin(angles)], axis=1).astype(jnp.bfloat16)

def rotate_phase(real_part, imag_part, channels, delay_values, fft_length):
    angles = 2.0 * math.pi / fft_length * channels * delay_values
    cosine = jnp.cos(angles)
    sine_part = jnp.sin(angles)
    factor = 1.0 / math.sqrt(fft_length)
    return ((real_part * cosine + imag_part * sine_part) * factor, (imag_part * cosine - real_part * sine_part) * factor)

def reference(voltages, filter_taps, delays, channel_flags):
    dft_table = build_table(NFFT).astype(jnp.float32)
    channels = jnp.arange(CHANNEL_COUNT).astype(jnp.float32)[:, None]

    def one_input(operands):
        samples, delay_value = operands
        frames = samples.reshape(S_TOT, NFFT).astype(jnp.float32)
        padded = jnp.concatenate([jnp.zeros((TAPS - 1, NFFT), jnp.float32), frames], axis=0)
        filtered = filter_taps[0] * padded[TAPS - 1:TAPS - 1 + S_TOT]
        for tap_index in range(1, TAPS):
            filtered = filtered + filter_taps[tap_index] * padded[TAPS - 1 - tap_index:TAPS - 1 - tap_index + S_TOT]
        filtered = lax.optimization_barrier(filtered.astype(jnp.bfloat16)).astype(jnp.float32)
        raw_spectra = jnp.einsum('cpn,sn->cps', dft_table, filtered, precision=lax.Precision.HIGHEST)
        real_part, imag_part = rotate_phase(raw_spectra[:, 0], raw_spectra[:, 1], channels, delay_value, NFFT)
        return jnp.stack([real_part, imag_part], axis=1).astype(jnp.bfloat16)
    spectra = lax.map(one_input, (voltages, delays))
    upper_mask = jnp.arange(NI)[:, None] <= jnp.arange(NI)[None, :]

    def one_channel(channel_index):
        channel_slab = lax.dynamic_index_in_dim(spectra, channel_index, axis=1, keepdims=False)
        direct = channel_slab.reshape(NI, 2 * S_TOT).astype(jnp.float32)
        swapped = jnp.concatenate([channel_slab[:, 1], -channel_slab[:, 0]], axis=1).astype(jnp.float32)
        real_gram = jnp.dot(direct, direct.T, precision=lax.Precision.HIGHEST)
        imag_gram = jnp.dot(swapped, direct.T, precision=lax.Precision.HIGHEST)
        packed = jnp.where(upper_mask, real_gram, imag_gram) / S_TOT
        flag_value = lax.dynamic_index_in_dim(channel_flags, channel_index, keepdims=False)
        return packed * flag_value.astype(jnp.float32)
    return lax.map(one_channel, jnp.arange(CHANNEL_COUNT, dtype=jnp.int32))
```

```python
import functools
import math

import jax
import jax.numpy as jnp
import numpy as np
from jax import lax
from jax.experimental import pallas as pl
from jax.experimental.pallas import tpu as pltpu
from jax.sharding import PartitionSpec as P

VMEM_LIMIT = 56 * 1024 * 1024
SEND_PEAK = 16384.0


def passed_along(block, axis, distance):
    devices = range(lax.axis_size(axis))
    route = [(i - distance, i) for i in devices if i - distance in devices]
    return lax.ppermute(block, axis, route)


def table_rows(channels, fft_length):
    samples = np.arange(fft_length, dtype=np.int64)
    product = channels[:, None].astype(np.int64) * samples[None, :] % fft_length
    angles = product.astype(np.float32) * np.float32(2.0 * math.pi / fft_length)
    rows = np.concatenate([np.cos(angles), -np.sin(angles)], axis=0)
    return rows.astype(jnp.bfloat16)


def dft_kernel(table_ref, cos_ref, sin_ref, filtered_ref, out_ref, *turned):
    inputs, frames = filtered_ref.shape[0], filtered_ref.shape[1]
    rows = table_ref.shape[0] // 2
    width = 128
    for i in range(inputs):
        raw = lax.dot_general(
            table_ref[...], filtered_ref[i], (((1,), (1,)), ((), ())),
            preferred_element_type=jnp.float32,
        )
        real, imag = raw[:rows], raw[rows:]
        cosine = cos_ref[0, :, i : i + 1]
        sine = sin_ref[0, :, i : i + 1]
        both = (real * cosine + imag * sine, imag * cosine - real * sine)
        for q in range(2):
            for piece in range(frames // width):
                turned[q * (frames // width) + piece][pl.ds(i, rows, stride=inputs), :] = both[q][
                    :, piece * width : (piece + 1) * width
                ]
    for piece, ref in enumerate(turned):
        value = ref[...].reshape(rows, inputs, width).astype(jnp.bfloat16)
        out_ref[:, :, piece * width : (piece + 1) * width] = value


def dft_call(table, cosine, sine, filtered):
    blocks, rows, inputs = cosine.shape
    inputs_here, frames, fft_length = filtered.shape
    out_shape = jax.ShapeDtypeStruct((rows, inputs_here, 2 * frames), jnp.bfloat16)
    return pl.pallas_call(
        dft_kernel,
        out_shape=out_shape,
        grid=(blocks,),
        in_specs=[
            pl.BlockSpec((2 * rows, fft_length), lambda b: (0, 0)),
            pl.BlockSpec((1, rows, inputs), lambda b: (b, 0, 0)),
            pl.BlockSpec((1, rows, inputs), lambda b: (b, 0, 0)),
            pl.BlockSpec((inputs, frames, fft_length), lambda b: (b, 0, 0)),
        ],
        out_specs=pl.BlockSpec((rows, inputs, 2 * frames), lambda b: (0, b, 0)),
        scratch_shapes=[pltpu.VMEM((rows * inputs, 128), jnp.float32)] * (2 * frames // 128),
        compiler_params=pltpu.CompilerParams(vmem_limit_bytes=VMEM_LIMIT),
        cost_estimate=pl.CostEstimate(
            flops=4 * rows * inputs_here * frames * fft_length,
            bytes_accessed=2 * inputs_here * frames * (fft_length + 2 * rows),
            transcendentals=0,
        ),
    )(table, cosine, sine, filtered)


def gram_kernel(frame_total, spectra_ref, vis_ref, peak_ref):
    sources, channels, inputs_here, columns = spectra_ref.shape
    total = sources * inputs_here
    half = columns // 2
    row = lax.broadcasted_iota(jnp.int32, (total, total), 0)
    column = lax.broadcasted_iota(jnp.int32, (total, total), 1)
    dims = (((1,), (1,)), ((), ()))
    for c in range(channels):
        slab = spectra_ref[:, c]
        if inputs_here % 16:
            slab = slab.astype(jnp.float32).reshape(total, columns).astype(jnp.bfloat16)
        else:
            slab = slab.reshape(total, columns)
        swapped = jnp.concatenate([slab[:, half:], -slab[:, :half]], axis=1)
        real = lax.dot_general(slab, slab, dims, preferred_element_type=jnp.float32)
        imag = lax.dot_general(swapped, slab, dims, preferred_element_type=jnp.float32)
        packed = jnp.where(row <= column, real, imag)
        peak = jnp.max(jnp.where(row == column, real, 0.0), axis=(0, 1), keepdims=True)
        peak = jnp.maximum(peak, 1e-30)
        vis_ref[c] = (packed * (SEND_PEAK / peak)).astype(vis_ref.dtype)
        peak_ref[c] = jnp.broadcast_to(peak * (1.0 / (SEND_PEAK * frame_total)), (8, 128))


def gram_call(spectra, frame_total):
    sources, channels, inputs_here, columns = spectra.shape
    total = sources * inputs_here
    step = 2 if channels % 2 == 0 else 1
    return pl.pallas_call(
        functools.partial(gram_kernel, frame_total),
        out_shape=(
            jax.ShapeDtypeStruct((channels, total, total), jnp.float32),
            jax.ShapeDtypeStruct((channels, 8, 128), jnp.float32),
        ),
        grid=(channels // step,),
        in_specs=[pl.BlockSpec((sources, step, inputs_here, columns), lambda b: (0, b, 0, 0))],
        out_specs=(
            pl.BlockSpec((step, total, total), lambda b: (b, 0, 0)),
            pl.BlockSpec((step, 8, 128), lambda b: (b, 0, 0)),
        ),
        compiler_params=pltpu.CompilerParams(vmem_limit_bytes=VMEM_LIMIT),
        cost_estimate=pl.CostEstimate(
            flops=4 * channels * total * total * columns,
            bytes_accessed=2 * channels * total * (columns + total),
            transcendentals=0,
        ),
    )(spectra)


def filter_frames(voltages, filter_taps):
    inputs_here, sample_count = voltages.shape
    tap_count, fft_length = filter_taps.shape
    local_frame_count = sample_count // fft_length
    frames = voltages.reshape(inputs_here, local_frame_count, fft_length)
    tail = voltages[:, sample_count - (tap_count - 1) * fft_length :]
    history = passed_along(tail, "tm", 1).reshape(inputs_here, tap_count - 1, fft_length)
    extended = jnp.concatenate([history, frames], axis=1).astype(jnp.float32)
    filtered = filter_taps[0] * extended[:, tap_count - 1 : tap_count - 1 + local_frame_count]
    for tap_index in range(1, tap_count):
        offset = tap_count - 1 - tap_index
        filtered = (
            filtered + filter_taps[tap_index] * extended[:, offset : offset + local_frame_count]
        )
    return filtered.astype(jnp.bfloat16)


def on_device(voltages, filter_taps, delays, channel_flags):
    inputs_here = voltages.shape[0]
    fft_length = filter_taps.shape[1]
    feeds, times = lax.axis_size("feed"), lax.axis_size("tm")
    filtered = filter_frames(voltages, filter_taps)
    frame_total = filtered.shape[1] * times
    owned = channel_flags.shape[0]
    kept = owned // times
    chunks = 4 if kept % 4 == 0 else 1
    width = kept // chunks
    block = 16 if inputs_here % 16 == 0 else inputs_here

    local_flags = lax.dynamic_slice_in_dim(
        channel_flags, lax.axis_index("tm") * kept, kept, 0
    ).astype(jnp.float32)
    scale = 1.0 / math.sqrt(fft_length)
    order = np.arange(feeds * owned).reshape(feeds, times, chunks, width)
    results = []
    for k in range(chunks):
        channels = order[:, :, k].reshape(-1)
        table = jnp.asarray(table_rows(channels, fft_length))
        angles = 2.0 * math.pi / fft_length * jnp.asarray(channels, jnp.float32)[None, :, None]
        angles = angles * delays.reshape(-1, 1, block)
        spectra = dft_call(table, jnp.cos(angles) * scale, jnp.sin(angles) * scale, filtered)
        spectra = spectra.reshape(feeds, times * width, inputs_here, spectra.shape[2])
        turned = lax.all_to_all(spectra, "feed", split_axis=0, concat_axis=0, tiled=True)
        vis, peak = gram_call(turned, frame_total)
        vis = vis.astype(jnp.float16).reshape(times, width, vis.shape[1], vis.shape[2])
        vis = lax.all_to_all(vis, "tm", split_axis=0, concat_axis=0, tiled=True)
        peak = lax.all_gather(peak[:, 0, 0], "tm", axis=0)
        peak = lax.dynamic_slice_in_dim(peak, lax.axis_index("tm") * width, width, 1)
        flags = local_flags[k * width : (k + 1) * width]
        total = jnp.sum(vis.astype(jnp.float32) * peak[:, :, None, None], axis=0)
        results.append(total * flags[:, None, None])
    return jnp.concatenate(results, axis=0)


def solution(mesh):
    in_specs = (P("feed", "tm"), P(), P("feed"), P("feed"))
    out_specs = P(("feed", "tm"), None, None)
    return jax.shard_map(
        on_device, mesh=mesh, in_specs=in_specs, out_specs=out_specs, check_vma=False
    )
```

```python
import functools
import math

import jax
import jax.numpy as jnp
import numpy as np
from jax import lax
from jax.experimental import pallas as pl
from jax.experimental.pallas import tpu as pltpu
from jax.sharding import PartitionSpec as P

VMEM_LIMIT = 56 * 1024 * 1024
SEND_PEAK = 16384.0
EXTRA_ROWS = 8


def passed_along(block, axis, distance):
    devices = range(lax.axis_size(axis))
    route = [(i - distance, i) for i in devices if i - distance in devices]
    return lax.ppermute(block, axis, route)


def table_rows(channels, fft_length):
    samples = np.arange(fft_length, dtype=np.int64)
    product = channels[:, None].astype(np.int64) * samples[None, :] % fft_length
    angles = product.astype(np.float32) * np.float32(2.0 * math.pi / fft_length)
    rows = np.concatenate([np.cos(angles), -np.sin(angles)], axis=0)
    return rows.astype(jnp.bfloat16)


def dft_kernel(table_ref, cos_ref, sin_ref, filtered_ref, out_ref, *turned):
    inputs, frames = filtered_ref.shape[0], filtered_ref.shape[1]
    rows = table_ref.shape[0] // 2
    width = 128
    for i in range(inputs):
        raw = lax.dot_general(
            table_ref[...], filtered_ref[i], (((1,), (1,)), ((), ())),
            preferred_element_type=jnp.float32,
        )
        real, imag = raw[:rows], raw[rows:]
        cosine = cos_ref[0, :, i : i + 1]
        sine = sin_ref[0, :, i : i + 1]
        both = (real * cosine + imag * sine, imag * cosine - real * sine)
        for q in range(2):
            for piece in range(frames // width):
                turned[q * (frames // width) + piece][pl.ds(i, rows, stride=inputs), :] = both[q][
                    :, piece * width : (piece + 1) * width
                ]
    for piece, ref in enumerate(turned):
        value = ref[...].reshape(rows, inputs, width).astype(jnp.bfloat16)
        out_ref[:, :, piece * width : (piece + 1) * width] = value


def dft_call(table, cosine, sine, filtered):
    blocks, rows, inputs = cosine.shape
    inputs_here, frames, fft_length = filtered.shape
    out_shape = jax.ShapeDtypeStruct((rows, inputs_here, 2 * frames), jnp.bfloat16)
    return pl.pallas_call(
        dft_kernel,
        out_shape=out_shape,
        grid=(blocks,),
        in_specs=[
            pl.BlockSpec((2 * rows, fft_length), lambda b: (0, 0)),
            pl.BlockSpec((1, rows, inputs), lambda b: (b, 0, 0)),
            pl.BlockSpec((1, rows, inputs), lambda b: (b, 0, 0)),
            pl.BlockSpec((inputs, frames, fft_length), lambda b: (b, 0, 0)),
        ],
        out_specs=pl.BlockSpec((rows, inputs, 2 * frames), lambda b: (0, b, 0)),
        scratch_shapes=[pltpu.VMEM((rows * inputs, 128), jnp.float32)] * (2 * frames // 128),
        compiler_params=pltpu.CompilerParams(vmem_limit_bytes=VMEM_LIMIT),
        cost_estimate=pl.CostEstimate(
            flops=4 * rows * inputs_here * frames * fft_length,
            bytes_accessed=2 * inputs_here * frames * (fft_length + 2 * rows),
            transcendentals=0,
        ),
    )(table, cosine, sine, filtered)


def gram_kernel(spectra_ref, vis_ref):
    sources, channels, inputs_here, columns = spectra_ref.shape
    total = sources * inputs_here
    half = columns // 2
    row = lax.broadcasted_iota(jnp.int32, (total, total), 0)
    column = lax.broadcasted_iota(jnp.int32, (total, total), 1)
    dims = (((1,), (1,)), ((), ()))
    for c in range(channels):
        slab = spectra_ref[:, c]
        if inputs_here % 16:
            slab = slab.astype(jnp.float32).reshape(total, columns).astype(jnp.bfloat16)
        else:
            slab = slab.reshape(total, columns)
        swapped = jnp.concatenate([slab[:, half:], -slab[:, :half]], axis=1)
        real = lax.dot_general(slab, slab, dims, preferred_element_type=jnp.float32)
        imag = lax.dot_general(swapped, slab, dims, preferred_element_type=jnp.float32)
        packed = jnp.where(row <= column, real, imag)
        peak = jnp.max(jnp.where(row == column, real, 0.0), axis=(0, 1), keepdims=True)
        peak = jnp.maximum(peak, 1e-30)
        power = jnp.ceil(jnp.log2(peak))
        vis_ref[c, :total] = packed * (SEND_PEAK * jnp.exp2(-power))
        vis_ref[c, total:] = jnp.broadcast_to(power, (EXTRA_ROWS, total))


def gram_call(spectra):
    sources, channels, inputs_here, columns = spectra.shape
    total = sources * inputs_here
    step = 2 if channels % 2 == 0 else 1
    return pl.pallas_call(
        gram_kernel,
        out_shape=jax.ShapeDtypeStruct((channels, total + EXTRA_ROWS, total), jnp.float32),
        grid=(channels // step,),
        in_specs=[pl.BlockSpec((sources, step, inputs_here, columns), lambda b: (0, b, 0, 0))],
        out_specs=pl.BlockSpec((step, total + EXTRA_ROWS, total), lambda b: (b, 0, 0)),
        compiler_params=pltpu.CompilerParams(vmem_limit_bytes=VMEM_LIMIT),
        cost_estimate=pl.CostEstimate(
            flops=4 * channels * total * total * columns,
            bytes_accessed=2 * channels * total * (columns + 2 * total),
            transcendentals=0,
        ),
    )(spectra)


def filter_kernel(history_ref, taps_ref, block_ref, out_ref, carry, turned):
    tap_count, fft_length = taps_ref.shape
    inputs, group = out_ref.shape[0], out_ref.shape[1]
    kept = tap_count - 1

    @pl.when(pl.program_id(0) == 0)
    def _():
        carry[...] = history_ref[...]

    def piece(p, unused):
        lanes = pl.multiple_of(p * 128, 128)
        taps = [taps_ref[t : t + 1, pl.ds(lanes, 128)] for t in range(tap_count)]
        frames = [
            carry[:, pl.ds(pl.multiple_of(h * fft_length + lanes, 128), 128)].astype(jnp.float32)
            for h in range(kept)
        ]
        for m in range(group):
            start = pl.multiple_of(m * fft_length + lanes, 128)
            frames.append(block_ref[:, pl.ds(start, 128)].astype(jnp.float32))
            value = taps[0] * frames[-1]
            for t in range(1, tap_count):
                value = value + taps[t] * frames[-1 - t]
            turned[pl.ds(m, inputs, stride=group), :] = value
        result = turned[...].reshape(inputs, group, 128).astype(jnp.bfloat16)
        out_ref[:, :, pl.ds(lanes, 128)] = result
        return unused

    lax.fori_loop(0, fft_length // 128, piece, 0)
    carry[...] = block_ref[:, (group - kept) * fft_length :]


def filter_frames(voltages, filter_taps):
    inputs_here, sample_count = voltages.shape
    tap_count, fft_length = filter_taps.shape
    frames = sample_count // fft_length
    kept = (tap_count - 1) * fft_length
    group = 16
    history = passed_along(voltages[:, sample_count - kept :], "tm", 1)
    return pl.pallas_call(
        filter_kernel,
        out_shape=jax.ShapeDtypeStruct((inputs_here, frames, fft_length), jnp.bfloat16),
        grid=(frames // group,),
        in_specs=[
            pl.BlockSpec((inputs_here, kept), lambda b: (0, 0)),
            pl.BlockSpec((tap_count, fft_length), lambda b: (0, 0)),
            pl.BlockSpec((inputs_here, group * fft_length), lambda b: (0, b)),
        ],
        out_specs=pl.BlockSpec((inputs_here, group, fft_length), lambda b: (0, b, 0)),
        scratch_shapes=[
            pltpu.VMEM((inputs_here, kept), jnp.bfloat16),
            pltpu.VMEM((inputs_here * group, 128), jnp.float32),
        ],
        compiler_params=pltpu.CompilerParams(vmem_limit_bytes=VMEM_LIMIT),
        cost_estimate=pl.CostEstimate(
            flops=8 * inputs_here * sample_count,
            bytes_accessed=4 * inputs_here * sample_count,
            transcendentals=0,
        ),
    )(history, filter_taps, voltages)


def on_device(voltages, filter_taps, delays, channel_flags):
    inputs_here = voltages.shape[0]
    fft_length = filter_taps.shape[1]
    feeds, times = lax.axis_size("feed"), lax.axis_size("tm")
    filtered = filter_frames(voltages, filter_taps)
    frame_total = filtered.shape[1] * times
    owned = channel_flags.shape[0]
    kept = owned // times
    chunks = 4 if kept % 4 == 0 else 1
    width = kept // chunks
    block = 16 if inputs_here % 16 == 0 else inputs_here

    local_flags = lax.dynamic_slice_in_dim(
        channel_flags, lax.axis_index("tm") * kept, kept, 0
    ).astype(jnp.float32)
    scale = 1.0 / math.sqrt(fft_length)
    order = np.arange(feeds * owned).reshape(feeds, times, chunks, width)
    place = lax.axis_index("tm")
    results = []
    sent = []
    for k in range(chunks):
        channels = order[:, :, k].reshape(-1)
        table = jnp.asarray(table_rows(channels, fft_length))
        angles = 2.0 * math.pi / fft_length * jnp.asarray(channels, jnp.float32)[None, :, None]
        angles = angles * delays.reshape(-1, 1, block)
        if k >= 2:
            filtered, sent[k - 2] = lax.optimization_barrier((filtered, sent[k - 2]))
        spectra = dft_call(table, jnp.cos(angles) * scale, jnp.sin(angles) * scale, filtered)
        spectra = spectra.reshape(feeds, times * width, inputs_here, spectra.shape[2])
        turned = lax.all_to_all(spectra, "feed", split_axis=0, concat_axis=0, tiled=True)
        vis = gram_call(turned).astype(jnp.float16)
        sent.append(vis.reshape(times, width, vis.shape[1], vis.shape[2]))
    for k in range(chunks):
        flags = local_flags[k * width : (k + 1) * width] * (1.0 / (SEND_PEAK * frame_total))
        total = 0.0
        for shift in range(times):
            target = lax.rem(place + shift, times)
            part = lax.dynamic_index_in_dim(sent[k], target, 0, keepdims=False)
            if shift:
                route = [(i, (i + shift) % times) for i in range(times)]
                part = lax.ppermute(part, "tm", route)
            part = part.astype(jnp.float32)
            count = part.shape[2]
            total = total + part[:, :count] * jnp.exp2(part[:, count:, :1][:, :1])
        results.append(total * flags[:, None, None])
    return jnp.concatenate(results, axis=0)


def solution(mesh):
    in_specs = (P("feed", "tm"), P(), P("feed"), P("feed"))
    out_specs = P(("feed", "tm"), None, None)
    return jax.shard_map(
        on_device, mesh=mesh, in_specs=in_specs, out_specs=out_specs, check_vma=False
    )
```

```python
import functools
import math

import jax
import jax.numpy as jnp
import numpy as np
from jax import lax
from jax.experimental import pallas as pl
from jax.experimental.pallas import tpu as pltpu
from jax.sharding import PartitionSpec as P

VMEM_LIMIT = 56 * 1024 * 1024
SEND_PEAK = 16384.0
EXTRA_ROWS = 8


def passed_along(block, axis, distance):
    devices = range(lax.axis_size(axis))
    route = [(i - distance, i) for i in devices if i - distance in devices]
    return lax.ppermute(block, axis, route)


def table_rows(channels, fft_length):
    samples = np.arange(fft_length, dtype=np.int64)
    product = channels[:, None].astype(np.int64) * samples[None, :] % fft_length
    angles = product.astype(np.float32) * np.float32(2.0 * math.pi / fft_length)
    rows = np.concatenate([np.cos(angles), -np.sin(angles)], axis=0)
    return rows.astype(jnp.bfloat16)


def dft_kernel(table_ref, cos_ref, sin_ref, filtered_ref, out_ref, *turned):
    inputs, frames = filtered_ref.shape[0], filtered_ref.shape[1]
    rows = table_ref.shape[0] // 2
    width = 128
    for i in range(inputs):
        raw = lax.dot_general(
            table_ref[...], filtered_ref[i], (((1,), (1,)), ((), ())),
            preferred_element_type=jnp.float32,
        )
        real, imag = raw[:rows], raw[rows:]
        cosine = cos_ref[0, :, i : i + 1]
        sine = sin_ref[0, :, i : i + 1]
        both = (real * cosine + imag * sine, imag * cosine - real * sine)
        for q in range(2):
            for piece in range(frames // width):
                turned[q * (frames // width) + piece][pl.ds(i, rows, stride=inputs), :] = both[q][
                    :, piece * width : (piece + 1) * width
                ]
    for piece, ref in enumerate(turned):
        value = ref[...].reshape(rows, inputs, width).astype(jnp.bfloat16)
        out_ref[:, :, piece * width : (piece + 1) * width] = value


def dft_call(table, cosine, sine, filtered):
    blocks, rows, inputs = cosine.shape
    inputs_here, frames, fft_length = filtered.shape
    out_shape = jax.ShapeDtypeStruct((rows, inputs_here, 2 * frames), jnp.bfloat16)
    return pl.pallas_call(
        dft_kernel,
        out_shape=out_shape,
        grid=(blocks,),
        in_specs=[
            pl.BlockSpec((2 * rows, fft_length), lambda b: (0, 0)),
            pl.BlockSpec((1, rows, inputs), lambda b: (b, 0, 0)),
            pl.BlockSpec((1, rows, inputs), lambda b: (b, 0, 0)),
            pl.BlockSpec((inputs, frames, fft_length), lambda b: (b, 0, 0)),
        ],
        out_specs=pl.BlockSpec((rows, inputs, 2 * frames), lambda b: (0, b, 0)),
        scratch_shapes=[pltpu.VMEM((rows * inputs, 128), jnp.float32)] * (2 * frames // 128),
        compiler_params=pltpu.CompilerParams(vmem_limit_bytes=VMEM_LIMIT),
        cost_estimate=pl.CostEstimate(
            flops=10 * 4 * rows * inputs_here * frames * fft_length,
            bytes_accessed=2 * inputs_here * frames * (fft_length + 2 * rows),
            transcendentals=0,
        ),
    )(table, cosine, sine, filtered)


def gram_kernel(spectra_ref, vis_ref):
    sources, channels, inputs_here, columns = spectra_ref.shape
    total = sources * inputs_here
    half = columns // 2
    row = lax.broadcasted_iota(jnp.int32, (total, total), 0)
    column = lax.broadcasted_iota(jnp.int32, (total, total), 1)
    dims = (((1,), (1,)), ((), ()))
    for c in range(channels):
        slab = spectra_ref[:, c]
        if inputs_here % 16:
            slab = slab.astype(jnp.float32).reshape(total, columns).astype(jnp.bfloat16)
        else:
            slab = slab.reshape(total, columns)
        swapped = jnp.concatenate([slab[:, half:], -slab[:, :half]], axis=1)
        real = lax.dot_general(slab, slab, dims, preferred_element_type=jnp.float32)
        imag = lax.dot_general(swapped, slab, dims, preferred_element_type=jnp.float32)
        packed = jnp.where(row <= column, real, imag)
        peak = jnp.max(jnp.where(row == column, real, 0.0), axis=(0, 1), keepdims=True)
        peak = jnp.maximum(peak, 1e-30)
        power = jnp.ceil(jnp.log2(peak))
        vis_ref[c, :total] = packed * (SEND_PEAK * jnp.exp2(-power))
        vis_ref[c, total:] = jnp.broadcast_to(power, (EXTRA_ROWS, total))


def gram_call(spectra):
    sources, channels, inputs_here, columns = spectra.shape
    total = sources * inputs_here
    step = 2 if channels % 2 == 0 else 1
    return pl.pallas_call(
        gram_kernel,
        out_shape=jax.ShapeDtypeStruct((channels, total + EXTRA_ROWS, total), jnp.float32),
        grid=(channels // step,),
        in_specs=[pl.BlockSpec((sources, step, inputs_here, columns), lambda b: (0, b, 0, 0))],
        out_specs=pl.BlockSpec((step, total + EXTRA_ROWS, total), lambda b: (b, 0, 0)),
        compiler_params=pltpu.CompilerParams(vmem_limit_bytes=VMEM_LIMIT),
        cost_estimate=pl.CostEstimate(
            flops=40 * 4 * channels * total * total * columns,
            bytes_accessed=2 * channels * total * (columns + 2 * total),
            transcendentals=0,
        ),
    )(spectra)


def filter_kernel(history_ref, taps_ref, block_ref, out_ref, carry, turned):
    tap_count, fft_length = taps_ref.shape
    inputs, group = out_ref.shape[0], out_ref.shape[1]
    kept = tap_count - 1

    @pl.when(pl.program_id(0) == 0)
    def _():
        carry[...] = history_ref[...]

    def piece(p, unused):
        lanes = pl.multiple_of(p * 128, 128)
        taps = [taps_ref[t : t + 1, pl.ds(lanes, 128)] for t in range(tap_count)]
        frames = [
            carry[:, pl.ds(pl.multiple_of(h * fft_length + lanes, 128), 128)].astype(jnp.float32)
            for h in range(kept)
        ]
        for m in range(group):
            start = pl.multiple_of(m * fft_length + lanes, 128)
            frames.append(block_ref[:, pl.ds(start, 128)].astype(jnp.float32))
            value = taps[0] * frames[-1]
            for t in range(1, tap_count):
                value = value + taps[t] * frames[-1 - t]
            turned[pl.ds(m, inputs, stride=group), :] = value
        result = turned[...].reshape(inputs, group, 128).astype(jnp.bfloat16)
        out_ref[:, :, pl.ds(lanes, 128)] = result
        return unused

    lax.fori_loop(0, fft_length // 128, piece, 0)
    carry[...] = block_ref[:, (group - kept) * fft_length :]


def filter_frames(voltages, filter_taps):
    inputs_here, sample_count = voltages.shape
    tap_count, fft_length = filter_taps.shape
    frames = sample_count // fft_length
    kept = (tap_count - 1) * fft_length
    group = 16
    history = passed_along(voltages[:, sample_count - kept :], "tm", 1)
    return pl.pallas_call(
        filter_kernel,
        out_shape=jax.ShapeDtypeStruct((inputs_here, frames, fft_length), jnp.bfloat16),
        grid=(frames // group,),
        in_specs=[
            pl.BlockSpec((inputs_here, kept), lambda b: (0, 0)),
            pl.BlockSpec((tap_count, fft_length), lambda b: (0, 0)),
            pl.BlockSpec((inputs_here, group * fft_length), lambda b: (0, b)),
        ],
        out_specs=pl.BlockSpec((inputs_here, group, fft_length), lambda b: (0, b, 0)),
        scratch_shapes=[
            pltpu.VMEM((inputs_here, kept), jnp.bfloat16),
            pltpu.VMEM((inputs_here * group, 128), jnp.float32),
        ],
        compiler_params=pltpu.CompilerParams(vmem_limit_bytes=VMEM_LIMIT),
        cost_estimate=pl.CostEstimate(
            flops=8 * inputs_here * sample_count,
            bytes_accessed=4 * inputs_here * sample_count,
            transcendentals=0,
        ),
    )(history, filter_taps, voltages)


def on_device(voltages, filter_taps, delays, channel_flags):
    inputs_here = voltages.shape[0]
    fft_length = filter_taps.shape[1]
    feeds, times = lax.axis_size("feed"), lax.axis_size("tm")
    filtered = filter_frames(voltages, filter_taps)
    frame_total = filtered.shape[1] * times
    owned = channel_flags.shape[0]
    kept = owned // times
    chunks = 4 if kept % 4 == 0 else 1
    width = kept // chunks
    block = 16 if inputs_here % 16 == 0 else inputs_here

    local_flags = lax.dynamic_slice_in_dim(
        channel_flags, lax.axis_index("tm") * kept, kept, 0
    ).astype(jnp.float32)
    flag_parts = (local_flags * (1.0 / (SEND_PEAK * frame_total))).reshape(chunks, width)
    scale = 1.0 / math.sqrt(fft_length)
    order = np.arange(feeds * owned).reshape(feeds, times, chunks, width)
    place = lax.axis_index("tm")

    def summed(vis, flags):
        total = 0.0
        for shift in range(times):
            target = lax.rem(place + shift, times)
            part = lax.dynamic_index_in_dim(vis, target, 0, keepdims=False)
            if shift:
                route = [(i, (i + shift) % times) for i in range(times)]
                part = lax.ppermute(part, "tm", route)
            part = part.astype(jnp.float32)
            count = part.shape[2]
            total = total + part[:, :count] * jnp.exp2(part[:, count:, :1][:, :1])
        return total * flags[:, None, None]

    results = []
    sent = []
    for k in range(chunks):
        channels = order[:, :, k].reshape(-1)
        table = jnp.asarray(table_rows(channels, fft_length))
        angles = 2.0 * math.pi / fft_length * jnp.asarray(channels, jnp.float32)[None, :, None]
        angles = angles * delays.reshape(-1, 1, block)
        if k >= 2:
            filtered, sent[k - 2] = lax.optimization_barrier((filtered, sent[k - 2]))
            results.append(summed(sent[k - 2], flag_parts[k - 2]))
        spectra = dft_call(table, jnp.cos(angles) * scale, jnp.sin(angles) * scale, filtered)
        spectra = spectra.reshape(feeds, times * width, inputs_here, spectra.shape[2])
        if k >= 3:
            spectra, results[k - 3] = lax.optimization_barrier((spectra, results[k - 3]))
        turned = lax.all_to_all(spectra, "feed", split_axis=0, concat_axis=0, tiled=True)
        if k >= 2:
            turned, results[k - 2] = lax.optimization_barrier((turned, results[k - 2]))
        vis = gram_call(turned).astype(jnp.float16)
        sent.append(vis.reshape(times, width, vis.shape[1], vis.shape[2]))
    for k in range(len(results), chunks):
        results.append(summed(sent[k], flag_parts[k]))
    return jnp.concatenate(results, axis=0)


def solution(mesh):
    in_specs = (P("feed", "tm"), P(), P("feed"), P("feed"))
    out_specs = P(("feed", "tm"), None, None)
    return jax.shard_map(
        on_device, mesh=mesh, in_specs=in_specs, out_specs=out_specs, check_vma=False
    )
```
